32 devices in a mesh: seq: 8 (over z, x), head: 4 (over y, core).
Axes of the slice: x: 2, y: 2, z: 4, core: 2. Of those that a mesh axis runs over, the one named last changes fastest.
Arguments:
- queries: bfloat16 [1024, 4096], P('seq', 'head'), may hold values from -250 to 250
- key_vectors: bfloat16 [1024, 512], P('seq', 'head'), may hold values from -250 to 250
- value_vectors: bfloat16 [1024, 512], P('seq', 'head'), may hold values from -20 to 20
- positions: int32 [1024], P('seq'), may hold values from 0 to 511, as said below
- query_map: float32 [32, 128, 128], P('head'), may hold values from -0.5 to 0.5
- key_map: float32 [4, 128, 128], P('head'), may hold values from -0.5 to 0.5
Outputs:
- grad_queries: float32 [1024, 4096], P('seq', 'head')
- grad_keys: float32 [1024, 512], P('seq', 'head')
- grad_values: float32 [1024, 512], P('seq', 'head')
- query_map_grad: float32 [32, 128, 128], P('head')
- key_map_grad: float32 [4, 128, 128], P('head')
The draws below stay inside these ranges and needn't reach their ends.
Inputs may be any that keep to these rules, and one draw needn't show every extreme that they name: positions[0] is 0, and each later position is either 0 (a document begins) or one more than the position before it; the slab holds at most 4 documents, and one of them is exactly 512 tokens long.
All inputs are finite; a program needn't handle non-finite values.
Results may differ from the reference program's by a relative error of at most 0.0025.
Values may be sent and summed in bfloat16 or wider, within the bound.
A program may use at most 64 MiB of HBM per device.

```python
import math
import jax
import jax.numpy as jnp
from jax import lax

HD = 128
GROUP = 8
FH = 128
TOK_DEV = 128
KV = 4
HEADS = 32
TOKENS = 1024


def attention_draw(key):
    base_key = jax.random.fold_in(key, 101)
    q_key, k_key = jax.random.split(base_key, 2)
    queries = jnp.clip(jax.random.normal(q_key, (TOKENS, KV, GROUP, HD), jnp.float32), -6.0, 6.0)
    key_rows = jnp.clip(jax.random.normal(k_key, (TOKENS, KV, HD), jnp.float32), -6.0, 6.0)
    queries = jnp.clip(queries, -250.0, 250.0).reshape(TOKENS, HEADS * HD)
    key_rows = jnp.clip(key_rows, -250.0, 250.0).reshape(TOKENS, KV * HD)
    return (queries, key_rows)


def draw_queries(key, part):
    return attention_draw(key)[0].astype(jnp.bfloat16)


def draw_key_vectors(key, part):
    return attention_draw(key)[1].astype(jnp.bfloat16)


def draw_value_vectors(key, part):
    noise_key, scale_key = jax.random.split(jax.random.fold_in(key, 23))
    noise = jnp.clip(jax.random.normal(noise_key, (TOKENS, KV, HD), jnp.float32), -6.0, 6.0)
    scales = jnp.exp(jax.random.uniform(scale_key, (KV,), jnp.float32, 0.0, math.log(3.0)))
    return (noise * scales[None, :, None]).reshape(TOKENS, KV * HD).astype(jnp.bfloat16)


def draw_positions(key, part):
    first_key, inner_key = jax.random.split(jax.random.fold_in(key, 5))
    half_len = TOKENS // 2
    first_cut = jax.random.randint(first_key, (), 1, half_len)
    inner_cut = jax.random.randint(inner_key, (), 1, jnp.maximum(first_cut, 2))
    cut_points = jnp.stack([inner_cut, first_cut, first_cut + half_len]).astype(jnp.int32)
    row_index = jnp.arange(TOKENS, dtype=jnp.int32)
    reached = cut_points[None, :] <= row_index[:, None]
    starts = jnp.max(jnp.where(reached, cut_points[None, :], 0), axis=1)
    return (row_index - starts).astype(jnp.int32)


def steps_of(own_key, extent, cuts, least, high):
    def one(dim, parts):
        heights = jax.random.uniform(jax.random.fold_in(jax.random.fold_in(own_key, 6), dim), (parts,), jnp.float32, least / len(cuts), high / len(cuts))
        return jnp.repeat(jnp.exp(heights), extent[dim] // parts).reshape((-1,) + (1,) * (len(extent) - dim - 1))

    gain = one(*cuts[0])
    for cut in cuts[1:]:
        gain = gain * one(*cut)
    return gain


def gaussian(own_key, shape, deviation, reach, cuts=(), held_as=jnp.bfloat16):
    values = jax.random.normal(own_key, shape, jnp.float32) * deviation
    if len(cuts) > 0:
        values = steps_of(own_key, shape, cuts, -0.22, 0.18) * values
    return jnp.clip(values, min=-reach, max=reach).astype(held_as)


def setup_inputs(seed: int = 0) -> dict:
    splits = jax.random.split(jax.random.key(seed), 7)
    queries = draw_queries(jax.random.fold_in(splits[6], 71), 0)
    key_vectors = draw_key_vectors(jax.random.fold_in(splits[6], 71), 0)
    value_vectors = draw_value_vectors(jax.random.fold_in(splits[6], 71), 0)
    positions = draw_positions(jax.random.fold_in(splits[6], 71), 0)
    query_map = gaussian(splits[4], (HEADS, HD, FH), HD ** -0.5, 0.5, ((0, 4),), jnp.float32)
    key_map = gaussian(splits[5], (KV, HD, FH), HD ** -0.5, 0.5, ((0, 4),), jnp.float32)
    return dict(queries=queries, key_vectors=key_vectors, value_vectors=value_vectors, positions=positions, query_map=query_map, key_map=key_map)


HIGHEST = lax.Precision.HIGHEST
NEGATIVE = -1e+30

def feature_map(logits):
    return jnp.concatenate([jax.nn.softmax(logits, axis=-1), jax.nn.softmax(-logits, axis=-1)], axis=-1)

def teacher_attention(queries, key_vectors, value_vectors, starts):
    q_heads = queries.astype(jnp.float32).reshape(TOKENS, KV, GROUP, HD)
    k_heads = key_vectors.astype(jnp.float32).reshape(TOKENS, KV, HD)
    v_heads = value_vectors.astype(jnp.float32).reshape(TOKENS, KV, HD)
    block_len = min(512, TOKENS)
    blocks = TOKENS // block_len
    scaling = 1.0 / math.sqrt(HD)

    def one_block(q_block):
        q_first = (q_block * block_len).astype(jnp.int32)
        q_part = lax.dynamic_slice_in_dim(q_heads, q_first, block_len, 0)
        s_part = lax.dynamic_slice_in_dim(starts, q_first, block_len, 0)
        q_index = q_first + jnp.arange(block_len, dtype=jnp.int32)

        def key_step(running, k_block):
            k_first = (k_block * block_len).astype(jnp.int32)

            def update(current):
                run_max, row_sum, summed = current
                k_part = lax.dynamic_slice_in_dim(k_heads, k_first, block_len, 0)
                v_part = lax.dynamic_slice_in_dim(v_heads, k_first, block_len, 0)
                k_index = k_first + jnp.arange(block_len, dtype=jnp.int32)
                visible = (k_index[None, :] <= q_index[:, None]) & (k_index[None, :] >= s_part[:, None])
                scores = jnp.einsum('tkgd,nkd->kgtn', q_part, k_part, precision=HIGHEST) * scaling
                scores = jnp.where(visible, scores, NEGATIVE)
                new_max = jnp.maximum(run_max, lax.optimization_barrier(jnp.max(scores, axis=-1)))
                weights = jnp.where(visible, jnp.exp(scores - new_max[..., None]), 0.0)
                fading = jnp.exp(run_max - new_max)
                row_sum = row_sum * fading + lax.optimization_barrier(jnp.sum(weights, axis=-1))
                rounded = lax.optimization_barrier(weights.astype(jnp.bfloat16)).astype(jnp.float32)
                summed = summed * fading[..., None] + jnp.einsum('kgtn,nkd->kgtd', rounded, v_part, precision=HIGHEST)
                return (new_max, row_sum, summed)
            return (lax.cond(k_first <= q_first + block_len - 1, update, lambda current: current, running), None)
        initial = (jnp.full((KV, GROUP, block_len), NEGATIVE, jnp.float32), jnp.zeros((KV, GROUP, block_len), jnp.float32), jnp.zeros((KV, GROUP, block_len, HD), jnp.float32))
        finals, unused = lax.scan(key_step, initial, jnp.arange(blocks, dtype=jnp.int32))
        return finals[2] / finals[1][..., None]
    outputs = lax.map(one_block, jnp.arange(blocks, dtype=jnp.int32))
    return jnp.transpose(outputs, (0, 3, 1, 2, 4)).reshape(TOKENS, KV, GROUP, HD)

def student(query_float, key_float, value_float, q_weights, k_weights, starts):
    q_logits = jnp.einsum('tkgd,kgdf->tkgf', query_float.reshape(TOKENS, KV, GROUP, HD), q_weights.reshape(KV, GROUP, HD, FH), precision=HIGHEST)
    query_phi = feature_map(q_logits)
    k_logits = jnp.einsum('tkd,kdf->tkf', key_float.reshape(TOKENS, KV, HD), k_weights, precision=HIGHEST)
    key_phi = feature_map(k_logits)
    v_heads = value_float.reshape(TOKENS, KV, HD)
    spans = TOKENS // TOK_DEV
    feat_width = 2 * FH
    inputs = (query_phi.reshape(spans, TOK_DEV, KV, GROUP, feat_width), key_phi.reshape(spans, TOK_DEV, KV, feat_width), v_heads.reshape(spans, TOK_DEV, KV, HD), starts.reshape(spans, TOK_DEV), jnp.arange(spans, dtype=jnp.int32) * TOK_DEV)

    def span_step(running, pieces):
        state_sum, norm_sums = running
        q_phi, k_phi, v_rows, s_rows, row_base = pieces
        row_index = row_base + jnp.arange(TOK_DEV, dtype=jnp.int32)
        visible = ((row_index[None, :] <= row_index[:, None]) & (row_index[None, :] >= s_rows[:, None])).astype(jnp.float32)
        crossing = (s_rows < row_base).astype(jnp.float32)
        inner = jnp.einsum('ikgf,jkf->kgij', q_phi, k_phi, precision=HIGHEST) * visible
        numer = jnp.einsum('kgij,jkd->ikgd', inner, v_rows, precision=HIGHEST)
        numer = numer + crossing[:, None, None, None] * jnp.einsum('ikgf,kfd->ikgd', q_phi, state_sum, precision=HIGHEST)
        denom = jnp.einsum('kgij->ikg', inner) + crossing[:, None, None] * jnp.einsum('ikgf,kf->ikg', q_phi, norm_sums, precision=HIGHEST)
        outputs = numer / denom[..., None]
        last_start = s_rows[-1]
        keeping = (s_rows == last_start).astype(jnp.float32)
        carried = (last_start < row_base).astype(jnp.float32)
        kept_phi = k_phi * keeping[:, None, None]
        state_sum = carried * state_sum + jnp.einsum('jkf,jkd->kfd', kept_phi, v_rows, precision=HIGHEST)
        norm_sums = carried * norm_sums + lax.optimization_barrier(jnp.sum(kept_phi, axis=0))
        return ((state_sum, norm_sums), outputs)
    initial = (jnp.zeros((KV, feat_width, HD), jnp.float32), jnp.zeros((KV, feat_width), jnp.float32))
    finals, outputs = lax.scan(span_step, initial, inputs)
    return outputs.reshape(TOKENS, KV, GROUP, HD)

def reference(queries, key_vectors, value_vectors, positions, query_map, key_map):
    starts = jnp.arange(TOKENS, dtype=jnp.int32) - positions.astype(jnp.int32)
    teacher = teacher_attention(queries, key_vectors, value_vectors, starts)

    def energy(query_float, key_float, value_float, q_weights, k_weights):
        outputs = student(query_float, key_float, value_float, q_weights, k_weights, starts)
        return 0.5 * jnp.sum((outputs - teacher) ** 2)
    grads = jax.grad(energy, argnums=(0, 1, 2, 3, 4))(queries.astype(jnp.float32), key_vectors.astype(jnp.float32), value_vectors.astype(jnp.float32), query_map, key_map)
    grad_norm = jnp.sqrt(jnp.sum(grads[3] * grads[3]) + jnp.sum(grads[4] * grads[4]))
    clip_limit = 0.25 * math.sqrt((HEADS + KV) * HD * FH)
    factor = jnp.minimum(1.0, clip_limit / (grad_norm + 1e-06))
    return (grads[0], grads[1], grads[2], factor * grads[3], factor * grads[4])
```

```python
import functools
import math

import jax
import jax.numpy as jnp
from jax import lax
from jax.experimental import pallas as pl
from jax.experimental.pallas import tpu as pltpu
from jax.sharding import PartitionSpec as P

F32 = jnp.float32
BF16 = jnp.bfloat16
NEGATIVE = -1e30
EPSILON = 1e-06
UNIT = 16
GRANT = 66_000_000
MESH = pl.DeviceIdType.MESH

NN = (((1,), (0,)), ((), ()))
NT = (((1,), (1,)), ((), ()))
TN = (((0,), (0,)), ((), ()))


def split(value):
    high = value.astype(BF16)
    low = (value - high.astype(F32)).astype(BF16)
    return (high, low)


def single(value):
    return (value.astype(BF16),)


def product(left, right, dims):
    total = lax.dot_general(left[0], right[0], dims, preferred_element_type=F32)
    if len(left) > 1:
        total = total + lax.dot_general(left[1], right[0], dims, preferred_element_type=F32)
    if len(right) > 1:
        total = total + lax.dot_general(left[0], right[1], dims, preferred_element_type=F32)
    return total


def softmax_pair(logits):
    up = jnp.exp(logits - jnp.max(logits, axis=-1, keepdims=True))
    low = jnp.exp(jnp.min(logits, axis=-1, keepdims=True) - logits)
    up = up / jnp.sum(up, axis=-1, keepdims=True)
    low = low / jnp.sum(low, axis=-1, keepdims=True)
    return jnp.concatenate([up, low], axis=-1)


def feature_back(phi, grad_phi, half):
    product_ = phi * grad_phi
    up, low = (product_[:, :half], product_[:, half:])
    up = up - phi[:, :half] * jnp.sum(up, axis=-1, keepdims=True)
    low = low - phi[:, half:] * jnp.sum(low, axis=-1, keepdims=True)
    return up - low


def kernel(
    count, heads, reach, batch, q_hbm, k_hbm, v_hbm, pos_hbm, qmap_hbm, kmap_hbm,
    gq_hbm, gk_hbm, gv_hbm, gqm_hbm, gkm_hbm,
    q_ref, pos_ref, qmap_ref, kmap_ref, load_s,
    gq_ref, gk_ref, gv_ref, gqm_ref, gkm_ref, store_s,
    win_k, win_v, bias, phi, inner_s, gn_s, gd_s, dlog_s, back_s, back_send, back_recv,
    past_s, q_loc, q_recv, q_all, q_own, k_loc, k_recv, k_all, norm_head, norm_seq,
    k_ss, k_rs, v_ss, v_rs, b_ss, b_rs, r_ss, r_rs, a_ss, a_rs, m_ss, m_rs, n_ss, n_rs, h_ss, h_rs, w_ss, w_rs,
):
    me = lax.axis_index("seq")
    my_head = lax.axis_index("head")
    rows, dim = k_hbm.shape
    group, _, half = qmap_ref.shape
    feat = 2 * half
    turns = group // batch
    parts = dim // UNIT
    span = batch * rows
    scaling = 1.0 / math.sqrt(dim)
    k_shard = k_loc.shape[1]
    owners = k_loc.shape[0]
    k_ref = win_k.at[pl.ds(reach * rows, rows)]
    v_ref = win_v.at[pl.ds(reach * rows, rows)]
    loads = [
        pltpu.make_async_copy(src, dst, load_s.at[i])
        for i, (src, dst) in enumerate(
            ((k_hbm, k_ref), (v_hbm, v_ref), (pos_hbm, pos_ref), (kmap_hbm, kmap_ref), (q_hbm, q_ref), (qmap_hbm, qmap_ref))
        )
    ]
    for load in loads:
        load.start()
    stores = [
        pltpu.make_async_copy(src, dst, store_s.at[i])
        for i, (src, dst) in enumerate(
            ((gq_ref, gq_hbm), (gk_ref, gk_hbm), (gv_ref, gv_hbm), (gqm_ref, gqm_hbm), (gkm_ref, gkm_hbm))
        )
    ]

    def owner_slot(h, part):
        unit = h * parts + part
        return (unit % count, unit // count)

    def remote(src, dst, send, recv, **where):
        return pltpu.make_async_remote_copy(
            src_ref=src, dst_ref=dst, send_sem=send, recv_sem=recv,
            device_id=where, device_id_type=MESH,
        )

    barrier = pltpu.get_barrier_semaphore()
    for step in range(1, count):
        pl.semaphore_signal(
            barrier, inc=1, device_id={"seq": lax.rem(me + step, count)}, device_id_type=MESH
        )
    for step in range(1, heads):
        pl.semaphore_signal(
            barrier, inc=1, device_id={"head": lax.rem(my_head + step, heads)}, device_id_type=MESH
        )
    loads[0].wait()
    loads[1].wait()
    pl.semaphore_wait(barrier, count + heads - 2)

    def block_copies(step):
        place = pl.ds((reach - step) * rows, rows)
        return (
            remote(k_ref, win_k.at[place], k_ss.at[step - 1], k_rs.at[step - 1], seq=lax.rem(me + step, count)),
            remote(v_ref, win_v.at[place], v_ss.at[step - 1], v_rs.at[step - 1], seq=lax.rem(me + step, count)),
        )

    for step in range(1, reach + 1):
        @pl.when(me + step < count)
        def _():
            for copy in block_copies(step):
                copy.start()

        @pl.when(me < step)
        def _():
            place = pl.ds((reach - step) * rows, rows)
            win_k[place, :] = jnp.zeros((rows, dim), BF16)
            win_v[place, :] = jnp.zeros((rows, dim), BF16)

    loads[2].wait()
    loads[3].wait()

    row_base = me * rows
    token = row_base + lax.broadcasted_iota(jnp.int32, (rows, rows), 0)
    positions = jnp.broadcast_to(pos_ref[...].astype(F32), (rows, rows)).T.astype(jnp.int32)
    starts = token - positions
    lane = lax.broadcasted_iota(jnp.int32, (rows, rows), 1)
    for slot in range(reach + 1):
        key_index = (me - reach + slot) * rows + lane
        seen = (key_index <= token) & (key_index >= starts)
        bias[:, slot * rows : (slot + 1) * rows] = jnp.where(seen, 0.0, NEGATIVE)
    own = jnp.where((row_base + lane <= token) & (row_base + lane >= starts), 1.0, 0.0)
    crossing = jnp.where(starts < row_base, 1.0, 0.0)[:, :1]
    keeping = jnp.where(starts == starts[rows - 1 :, :], 1.0, 0.0)[:, :1]
    first_start = starts[:1, :1]
    last_start = starts[rows - 1 :, :1]

    kmap = split(kmap_ref[0])
    key_phi = softmax_pair(product((k_ref[...],), kmap, NN))
    key_parts = split(key_phi)

    def features(turn, carry):
        for h in range(batch):
            g = turn * batch + h
            q = q_ref[:, pl.ds(pl.multiple_of(g * dim, dim), dim)]
            place = pl.ds(pl.multiple_of(g * rows, rows), rows)
            phi[place, :] = softmax_pair(product((q,), split(qmap_ref[g]), NN))
        return carry

    loads[4].wait()
    loads[5].wait()
    lax.fori_loop(0, group // batch, features, 0)

    for step in range(1, reach + 1):
        @pl.when(me >= step)
        def _():
            for copy in block_copies(step):
                copy.wait_recv()

    earlier = win_k[: reach * rows, :]
    past_phi = softmax_pair(product((earlier,), kmap, NN))
    past_index = (me - reach) * rows + lax.broadcasted_iota(jnp.int32, (reach * rows, 1), 0)
    past_phi = past_phi * jnp.where(past_index >= first_start, 1.0, 0.0)
    past_s[...] = past_phi
    state = product(split(past_phi), (win_v[: reach * rows, :],), TN)
    norms = jnp.sum(past_phi, axis=0, keepdims=True)
    state_parts = split(state)
    value = (v_ref[...],)

    back_s[...] = jnp.zeros_like(back_s)

    def stacked(part):
        return jnp.broadcast_to(part[None], (batch,) + part.shape).reshape(
            (batch * part.shape[0],) + part.shape[1:]
        )

    def forward(turn):
        place = pl.ds(turn * span, span)
        q = jnp.concatenate(
            [
                q_ref[:, (turn * batch + h) * dim : (turn * batch + h + 1) * dim]
                for h in range(batch)
            ],
            axis=0,
        )
        scores = lax.dot_general(q, win_k[...], NT, preferred_element_type=F32) * scaling
        scores = (scores.reshape(batch, rows, -1) + bias[...][None]).reshape(span, -1)
        weights = jnp.exp(scores - jnp.max(scores, axis=-1, keepdims=True))
        total = jnp.sum(weights, axis=-1, keepdims=True)
        teacher = lax.dot_general(weights.astype(BF16), win_v[...], NN, preferred_element_type=F32)
        teacher = teacher / total
        q_phi = phi[place, :]
        cross = stacked(crossing)
        crossed = q_phi * cross
        inner = product(split(q_phi), key_parts, NT) * stacked(own)
        crossed_parts = split(crossed)
        numer = product(split(inner), value, NN) + product(crossed_parts, state_parts, NN)
        denom = jnp.sum(inner, axis=-1, keepdims=True) + jnp.sum(
            crossed * norms, axis=-1, keepdims=True
        )
        student = numer / denom
        error = student - teacher
        grad_numer = error / denom
        grad_denom = -jnp.sum(error * student, axis=-1, keepdims=True) / denom
        inner_s[place, :] = inner
        gn_s[place, :] = grad_numer
        gd_s[place, :] = jnp.broadcast_to(grad_denom, (span, dim))
        back_s[:feat, :] += product(crossed_parts, split(grad_numer), TN)
        down = jnp.sum(crossed * grad_denom, axis=0, keepdims=True)
        back_s[feat : feat + 1, :] += down[:, :half]
        back_s[feat + 1 : feat + 2, :] += down[:, half:]

    def shard_copy(turn, target):
        return remote(q_loc.at[turn, target], q_recv.at[turn, me], r_ss.at[turn], r_rs.at[turn], seq=target)

    def backward(turn, carry):
        grad_kphi, grad_values = carry
        place = pl.ds(turn * span, span)
        q_phi = phi[place, :]
        grad_numer = split(gn_s[place, :])
        grad_denom = gd_s[place, :1]
        mixing = (product(grad_numer, value, NT) + grad_denom) * stacked(own)
        mixing = split(mixing)
        grad_qphi = product(mixing, key_parts, NN)
        grad_qphi = grad_qphi + stacked(crossing) * (
            product(grad_numer, state_parts, NT) + grad_denom * norms
        )
        dlog = feature_back(q_phi, grad_qphi, half)
        dlog_s[place, :] = dlog
        for h in range(batch):
            g = turn * batch + h
            q = q_ref[:, g * dim : (g + 1) * dim]
            grad_map = product((q,), split(dlog[h * rows : (h + 1) * rows]), TN)
            for part in range(parts):
                owner, slot = owner_slot(h, part)
                piece = grad_map[part * UNIT : (part + 1) * UNIT]
                q_loc[turn, owner, slot * UNIT : (slot + 1) * UNIT, :] = piece.astype(BF16)
                q_own[turn, owner, slot * UNIT : (slot + 1) * UNIT, :] = piece
        for step in range(1, count):
            shard_copy(turn, lax.rem(me + step, count)).start()
        grad_kphi = grad_kphi + product(mixing, split(q_phi), TN)
        grad_values = grad_values + product(split(inner_s[place, :]), grad_numer, TN)
        return (grad_kphi, grad_values)

    def back_copy(step):
        return remote(
            back_send, back_recv.at[step - 1], b_ss.at[step - 1], b_rs.at[step - 1],
            seq=lax.rem(me + count - step, count),
        )

    sums = (jnp.zeros((rows, feat), F32), jnp.zeros((rows, dim), F32))
    for turn in range(turns):
        forward(turn)
        sums = backward(turn, sums)
    grad_kphi, grad_values = sums

    down_parts = split(back_s[:feat, :])
    down_norms = jnp.concatenate([back_s[feat : feat + 1, :], back_s[feat + 1 : feat + 2, :]], axis=1)
    past_grad = product((win_v[: reach * rows, :],), down_parts, NT) + down_norms
    past_dlog = split(feature_back(past_s[...], past_grad, half))
    own_dlog = split(feature_back(key_phi, grad_kphi, half))
    key_grad = product((k_ref[...],), own_dlog, TN) + product((win_k[: reach * rows, :],), past_dlog, TN)
    for owner in range(owners):
        k_loc[owner] = key_grad[owner * k_shard : (owner + 1) * k_shard]

    def key_copy(target):
        return remote(k_loc.at[target], k_recv.at[me], n_ss.at[target], n_rs.at[me], seq=target)

    for owner in range(owners):
        @pl.when(owner != me)
        def _():
            key_copy(owner).start()

    origin = jnp.floor(first_start.astype(F32) * (1.0 / rows))
    back_s[feat + 8 :, :] = jnp.broadcast_to(origin, (back_s.shape[0] - feat - 8, dim))
    back_send[...] = back_s[...].astype(BF16)

    def gather(turn, step):
        return remote(
            q_all.at[turn, me], q_all.at[turn, me], a_ss.at[turn], a_rs.at[turn], seq=lax.rem(me + step, count)
        )

    def every(whole, turn, send, recv):
        place = whole.at[turn, pl.ds(0, count - 1)]
        return remote(place, place, send.at[turn], recv.at[turn], seq=lax.rem(me + 1, count))

    def reduced(turn):
        every(q_recv, turn, r_ss, r_rs).wait_recv()
        summed = q_own[turn, me]
        for step in range(1, count):
            summed = summed + q_recv[turn, lax.rem(me + step, count)].astype(F32)
        q_all[turn, me] = summed.astype(BF16)
        for step in range(1, count):
            gather(turn, step).start()
        return jnp.sum(summed * summed, axis=0, keepdims=True)

    squares = jnp.zeros((1, half), F32)
    for turn in range(turns - 1):
        squares = squares + reduced(turn)

    for step in range(1, reach + 1):
        @pl.when(me >= step)
        def _():
            back_copy(step).start()

    def to_queries(turn, carry):
        for h in range(batch):
            g = turn * batch + h
            place = pl.ds(pl.multiple_of(g * rows, rows), rows)
            gq_ref[:, pl.ds(pl.multiple_of(g * dim, dim), dim)] = product(
                split(dlog_s[place, :]), split(qmap_ref[g]), NT
            )
        return carry

    lax.fori_loop(0, turns, to_queries, 0)
    stores[0].start()

    squares = squares + reduced(turns - 1)
    norm_head[my_head] = squares

    @pl.when(me < owners)
    def _():
        key_sum = k_loc[lax.rem(me, owners)]
        for step in range(1, count):
            other = lax.rem(me + step, count)
            remote(k_loc.at[0], k_recv.at[other], n_ss.at[0], n_rs.at[other], seq=other).wait_recv()
            key_sum = key_sum + k_recv[other]
        k_all[lax.rem(me, owners)] = key_sum
        norm_head[my_head] = squares + jnp.sum(key_sum * key_sum, axis=0, keepdims=True)

    for step in range(1, heads):
        remote(
            norm_head.at[my_head], norm_head.at[my_head], h_ss.at[step], h_rs.at[my_head],
            head=lax.rem(my_head + step, heads),
        ).start()

    @pl.when(me < owners)
    def _():
        for step in range(1, count):
            spot = lax.rem(me, owners)
            remote(k_all.at[spot], k_all.at[spot], m_ss.at[step], m_rs.at[spot], seq=lax.rem(me + step, count)).start()

    for step in range(1, heads):
        other = lax.rem(my_head + step, heads)
        remote(norm_head.at[other], norm_head.at[other], h_ss.at[step], h_rs.at[other], head=other).wait_recv()
    total_squares = norm_head[0]
    for other in range(1, heads):
        total_squares = total_squares + norm_head[other]
    norm_seq[me] = total_squares
    for step in range(1, count):
        remote(
            norm_seq.at[me], norm_seq.at[me], w_ss.at[step], w_rs.at[me], seq=lax.rem(me + step, count)
        ).start()

    for step in range(1, reach + 1):
        @pl.when(me + step < count)
        def _():
            back_copy(step).wait_recv()

        @pl.when(me + step >= count)
        def _():
            back_recv[step - 1] = jnp.full(back_recv.shape[1:], 2.0 * count, BF16)

    mine = me.astype(F32)
    back = jnp.zeros((feat + 8, dim), F32)
    for step in range(1, reach + 1):
        arrived = back_recv[step - 1].astype(F32)
        back = back + jnp.where(arrived[feat + 8 : feat + 9, :1] <= mine, arrived[: feat + 8], 0.0)
    back_norms = jnp.concatenate([back[feat : feat + 1], back[feat + 1 : feat + 2]], axis=1)
    back_parts = single(back[:feat])
    grad_kphi = grad_kphi + keeping * (product(value, back_parts, NT) + back_norms)
    gv_ref[...] = grad_values + keeping * product(key_parts, back_parts, NN)
    gk_ref[...] = product(split(feature_back(key_phi, grad_kphi, half)), kmap, NT)
    stores[1].start()
    stores[2].start()

    for step in range(1, count):
        other = lax.rem(me + step, count)
        remote(norm_seq.at[other], norm_seq.at[other], w_ss.at[step], w_rs.at[other], seq=other).wait_recv()
    squares = norm_seq[0]
    for other in range(1, count):
        squares = squares + norm_seq[other]
    squared = jnp.sum(squares, axis=1, keepdims=True)
    limit = 0.25 * math.sqrt((group + 1) * heads * dim * half)
    factor = jnp.minimum(1.0, limit / (jnp.sqrt(squared) + EPSILON))
    for turn in range(turns):
        every(q_all, turn, a_ss, a_rs).wait_recv()
        for h in range(batch):
            for part in range(parts):
                owner, slot = owner_slot(h, part)
                first = (turn * batch + h) * dim + part * UNIT
                gqm_ref[first : first + UNIT, :] = factor * q_all[
                    turn, owner, slot * UNIT : (slot + 1) * UNIT, :
                ].astype(F32)
    stores[3].start()
    for owner in range(owners):
        @pl.when(owner != me)
        def _():
            remote(k_all.at[owner], k_all.at[owner], m_ss.at[0], m_rs.at[owner], seq=owner).wait_recv()
    gkm_ref[...] = factor * k_all[...].reshape(owners * k_shard, half)
    stores[4].start()

    for step in range(1, reach + 1):
        @pl.when(me + step < count)
        def _():
            for copy in block_copies(step):
                copy.wait_send()

        @pl.when(me >= step)
        def _():
            back_copy(step).wait_send()

    for turn in range(turns):
        every(q_loc, turn, r_ss, r_rs).wait_send()
        every(q_all, turn, a_ss, a_rs).wait_send()

    for step in range(1, count):
        remote(
            norm_seq.at[me], norm_seq.at[me], w_ss.at[step], w_rs.at[me], seq=lax.rem(me + step, count)
        ).wait_send()

        @pl.when(me < owners)
        def _():
            spot = lax.rem(me, owners)
            remote(k_all.at[spot], k_all.at[spot], m_ss.at[step], m_rs.at[spot], seq=lax.rem(me + step, count)).wait_send()

    for owner in range(owners):
        @pl.when(owner != me)
        def _():
            key_copy(owner).wait_send()

    for step in range(1, heads):
        remote(
            norm_head.at[my_head], norm_head.at[my_head], h_ss.at[step], h_rs.at[my_head],
            head=lax.rem(my_head + step, heads),
        ).wait_send()
    for store in stores:
        store.wait()


def finish(*refs):
    size = (len(refs) - 2) // 3
    sources, targets, held = (refs[:size], refs[size : 2 * size], refs[2 * size : 3 * size])
    incoming = [pltpu.make_async_copy(sources[i], held[i], refs[-2].at[i]) for i in range(size)]
    outgoing = [pltpu.make_async_copy(held[i], targets[i], refs[-1].at[i]) for i in range(size)]
    for copy in incoming:
        copy.start()
    for copy, after in zip(incoming, outgoing):
        copy.wait()
        after.start()
    for copy in outgoing:
        copy.wait()


def on_device(queries, key_vectors, value_vectors, positions, query_map, key_map):
    count = lax.axis_size("seq")
    heads = lax.axis_size("head")
    rows, dim = key_vectors.shape
    group, _, half = query_map.shape
    feat = 2 * half
    reach = max(1, count // 2)
    batch = min(group, max(2, UNIT * count // dim))
    turns = group // batch
    shard = batch * dim // count
    total = group * rows
    k_shard = max(8, dim // count)
    owners = dim // k_shard
    hbm = pl.BlockSpec(memory_space=pltpu.HBM)
    dma = pltpu.SemaphoreType.DMA
    outs = pl.pallas_call(
        functools.partial(kernel, count, heads, reach, batch),
        out_shape=(
            jax.ShapeDtypeStruct((rows, group * dim), F32),
            jax.ShapeDtypeStruct((rows, dim), F32),
            jax.ShapeDtypeStruct((rows, dim), F32),
            jax.ShapeDtypeStruct((group * dim, half), F32),
            jax.ShapeDtypeStruct((dim, half), F32),
        ),
        in_specs=[hbm] * 6,
        out_specs=(hbm,) * 5,
        scratch_shapes=[
            pltpu.VMEM((rows, group * dim), BF16),
            pltpu.VMEM((1, rows), jnp.int32),
            pltpu.VMEM(query_map.shape, F32),
            pltpu.VMEM(key_map.shape, F32),
            dma((6,)),
            pltpu.VMEM((rows, group * dim), F32),
            pltpu.VMEM((rows, dim), F32),
            pltpu.VMEM((rows, dim), F32),
            pltpu.VMEM((group * dim, half), F32),
            pltpu.VMEM((dim, half), F32),
            dma((5,)),
            pltpu.VMEM(((reach + 1) * rows, dim), BF16),
            pltpu.VMEM(((reach + 1) * rows, dim), BF16),
            pltpu.VMEM((rows, (reach + 1) * rows), F32),
            pltpu.VMEM((total, feat), F32),
            pltpu.VMEM((total, rows), F32),
            pltpu.VMEM((total, dim), F32),
            pltpu.VMEM((total, dim), F32),
            pltpu.VMEM((total, half), F32),
            pltpu.VMEM((feat + 16, dim), F32),
            pltpu.VMEM((feat + 16, dim), BF16),
            pltpu.VMEM((reach, feat + 16, dim), BF16),
            pltpu.VMEM((reach * rows, feat), F32),
            pltpu.VMEM((turns, count, shard, half), BF16),
            pltpu.VMEM((turns, count, shard, half), BF16),
            pltpu.VMEM((turns, count, shard, half), BF16),
            pltpu.VMEM((turns, count, shard, half), F32),
            pltpu.VMEM((owners, k_shard, half), F32),
            pltpu.VMEM((count, k_shard, half), F32),
            pltpu.VMEM((owners, k_shard, half), F32),
            pltpu.VMEM((heads, 1, half), F32),
            pltpu.VMEM((count, 1, half), F32),
            dma((reach,)), dma((reach,)), dma((reach,)), dma((reach,)), dma((reach,)), dma((reach,)),
            dma((turns,)), dma((turns,)), dma((turns,)), dma((turns,)), dma((count,)), dma((count,)),
            dma((count,)), dma((count,)), dma((heads,)), dma((heads,)), dma((count,)), dma((count,)),
        ],
        compiler_params=pltpu.CompilerParams(
            collective_id=0, has_side_effects=True, vmem_limit_bytes=GRANT
        ),
    )(queries, key_vectors, value_vectors, positions.reshape(1, rows), query_map, key_map)
    outs = pl.pallas_call(
        finish,
        out_shape=tuple(jax.ShapeDtypeStruct(out.shape, out.dtype) for out in outs),
        in_specs=[hbm] * 5,
        out_specs=(hbm,) * 5,
        scratch_shapes=[pltpu.VMEM(out.shape, out.dtype) for out in outs] + [dma((5,)), dma((5,))],
        compiler_params=pltpu.CompilerParams(vmem_limit_bytes=GRANT),
    )(*outs)
    return (
        outs[0], outs[1], outs[2],
        outs[3].reshape(group, dim, half), outs[4].reshape(1, dim, half),
    )


def solution(mesh):
    placed = (
        P("seq", "head"),
        P("seq", "head"),
        P("seq", "head"),
        P("seq"),
        P("head", None, None),
        P("head", None, None),
    )
    return jax.shard_map(
        on_device,
        mesh=mesh,
        in_specs=placed,
        out_specs=(
            P("seq", "head"),
            P("seq", "head"),
            P("seq", "head"),
            P("head", None, None),
            P("head", None, None),
        ),
        check_vma=False,
    )
```
